32 devices in a mesh: groups: 1, tm: 32 (over z, y, x, core).
Axes of the slice: x: 2, y: 2, z: 4, core: 2. Of those that a mesh axis runs over, the one named last changes fastest.
Arguments:
- latents: bfloat16 [32, 512, 512], P(('groups', 'tm')), may hold values from -21 to 21
- w_query: bfloat16 [512, 512], replicated, may hold values from -3 to 3
- w_key: bfloat16 [512, 512], replicated, may hold values from -3 to 3
- w_value: bfloat16 [512, 512], replicated, may hold values from -0.25 to 0.25
- w_out: bfloat16 [512, 512], replicated, may hold values from -0.25 to 0.25
- w_time: bfloat16 [3, 512, 512], replicated, may hold values from -0.15625 to 0.15625
- w_space: bfloat16 [3, 3, 512, 512], replicated, may hold values from -0.09375 to 0.09375
- tile_starts: int32 [4], P('groups'), may hold values from 0 to 25, as said below
Outputs:
- decoded: bfloat16 [32, 512, 512], P(('groups', 'tm'))
The draws below stay inside these ranges and needn't reach their ends.
Inputs may be any that keep to these rules, and one draw needn't show every extreme that they name: `tile_starts`: Increasing; the first is 0, the last is (3) * 8 + 1, and every other start t lies within 2 frames of t * 8.
All inputs are finite; a program needn't handle non-finite values.
Results may differ from the reference program's by a relative error of at most 0.0096.
Values may be sent and summed in bfloat16 or wider, within the bound.
A program may use at most 64 MiB of HBM per device.

```python
import math
import jax
import jax.numpy as jnp
from jax import lax

C = 512
PH = 16
PW = 32
TILE = 8
OV = 2
FRAMES = 32
POS = 512
NT = 4


def draw_latents(key, part):
    base_key = jax.random.fold_in(key, 21)
    keys = jax.random.split(base_key, 3)
    column = jnp.exp(jax.random.uniform(keys[0], (C,), jnp.float32, math.log(0.3), math.log(3.0)))
    rowwise = jnp.exp(jax.random.uniform(keys[1], (FRAMES, POS, 1), jnp.float32, math.log(0.5), math.log(2.0)))
    raw = jax.random.truncated_normal(keys[2], -3.0, 3.0, (FRAMES, POS, C), jnp.float32)
    scaled = raw * column * rowwise
    return scaled.astype(jnp.bfloat16)


def shared_query(key):
    raw = jax.random.truncated_normal(jax.random.fold_in(key, 31), -4.0, 4.0, (C, C), jnp.float32)
    return raw * C ** (-0.5)


def draw_w_query(key, part):
    return shared_query(key).astype(jnp.bfloat16)


def draw_w_key(key, part):
    raw = jax.random.truncated_normal(jax.random.fold_in(key, 32), -4.0, 4.0, (C, C), jnp.float32)
    return (raw * C ** (-0.5)).astype(jnp.bfloat16)


def draw_tile_starts(key, part):
    index = jnp.arange(NT).astype(jnp.int32)
    jitter = jax.random.randint(jax.random.fold_in(key, 41), (NT,), -2, 3).astype(jnp.int32)
    starts = index * TILE + jitter
    starts = jnp.where(index == NT - 1, index * TILE + 1, starts)
    starts = jnp.where(index == 0, 0, starts)
    return starts.astype(jnp.int32)


def normal_values(key, dims, width, most, held_as=jnp.bfloat16):
    drawn = jax.random.normal(key, dims, jnp.float32) * width
    return jnp.minimum(jnp.maximum(drawn, -most), most).astype(held_as)


def setup_inputs(seed: int = 0, part: int = 0) -> dict:
    key_list = jax.random.split(jax.random.key(seed), 9)
    part_keys = jax.random.split(jax.random.fold_in(key_list[8], part), 9)
    return {
        "latents": draw_latents(jax.random.fold_in(jax.random.fold_in(key_list[8], part), 71), part),
        "w_query": draw_w_query(jax.random.fold_in(key_list[8], 71), part),
        "w_key": draw_w_key(jax.random.fold_in(key_list[8], 71), part),
        "w_value": normal_values(key_list[3], (C, C), C ** -0.5, 0.25),
        "w_out": normal_values(key_list[4], (C, C), C ** -0.5, 0.25),
        "w_time": normal_values(key_list[5], (3, C, C), (3 * C) ** -0.5, 0.15625),
        "w_space": normal_values(key_list[6], (3, 3, C, C), (9 * C) ** -0.5, 0.09375),
        "tile_starts": draw_tile_starts(jax.random.fold_in(jax.random.fold_in(key_list[8], part), 71), part),
    }


epsilon = 1e-06

def rms_norm(array):
    wide = array.astype(jnp.float32)
    return (wide * lax.rsqrt(lax.optimization_barrier(jnp.mean(wide * wide, axis=-1, keepdims=True)) + epsilon)).astype(jnp.bfloat16)

def project(array, weight):
    extent = array.shape
    product = jnp.dot(array.reshape(-1, extent[-1]), weight, preferred_element_type=jnp.float32)
    return product.reshape(extent[:-1] + (weight.shape[-1],))

def tile_frames(frames, starts):
    reached = starts[None, :] <= frames[:, None]
    new_start = lax.optimization_barrier(jnp.max(jnp.where(reached, starts[None, :], 0), axis=1)).astype(jnp.int32)
    earlier = starts[None, :] < new_start[:, None]
    old_start = lax.optimization_barrier(jnp.max(jnp.where(earlier, starts[None, :], 0), axis=1)).astype(jnp.int32)
    inside = frames - new_start
    shared = jnp.logical_and(new_start > 0, inside < OV)
    fade = jnp.where(shared, (inside + 1).astype(jnp.float32) / float(OV + 1), jnp.float32(1.0))
    return (new_start, old_start, fade.astype(jnp.float32)[:, None, None])

def space_mix(blended, w_space):
    length = blended.shape[0]
    channels = blended.shape[-1]
    spatial = blended.reshape(length, PH, PW, channels)
    padded = jnp.pad(spatial, ((0, 0), (1, 1), (1, 1), (0, 0)))
    summed = jnp.zeros((length * PH * PW, channels), jnp.float32)
    for row_shift in range(3):
        for col_shift in range(3):
            window = padded[:, row_shift:row_shift + PH, col_shift:col_shift + PW].reshape(-1, channels)
            summed = summed + jnp.dot(window, w_space[row_shift, col_shift], preferred_element_type=jnp.float32)
    return summed.reshape(length, PH * PW, channels)

def reference(latents, w_query, w_key, w_value, w_out, w_time, w_space, tile_starts):
    normed = rms_norm(latents)
    queries = project(normed, w_query).astype(jnp.bfloat16)
    key_rows = project(normed, w_key).astype(jnp.bfloat16)
    values = project(normed, w_value).astype(jnp.bfloat16)
    scores = jnp.einsum('fpc,gpc->pfg', queries.astype(jnp.float32), key_rows.astype(jnp.float32)) * C ** (-0.5)
    order = jnp.arange(FRAMES)
    causal = order[:, None] >= order[None, :]
    scores = jnp.where(causal[None], scores, jnp.float32(-1e+30))
    peak = lax.optimization_barrier(jnp.max(scores, axis=-1, keepdims=True))
    expo = jnp.exp(scores - peak)
    weights = (expo / lax.optimization_barrier(jnp.sum(expo, axis=-1, keepdims=True))).astype(jnp.bfloat16)
    attended = jnp.einsum('pfg,gpc->fpc', weights.astype(jnp.float32), values.astype(jnp.float32)).astype(jnp.bfloat16)
    hidden = (latents.astype(jnp.float32) + project(attended, w_out)).astype(jnp.bfloat16)
    smooth = rms_norm(hidden)
    frames = jnp.arange(FRAMES).astype(jnp.int32)
    new_start, old_start, fade = tile_frames(frames, tile_starts)

    def mixed(context):
        summed = jnp.zeros(smooth.shape, jnp.float32)
        for lag_index in range(3):
            source = jnp.maximum(frames - lag_index, context).astype(jnp.int32)
            summed = summed + project(jnp.take(smooth, source, axis=0), w_time[lag_index])
        return summed
    blended = (fade * jax.nn.silu(mixed(new_start)) + (1.0 - fade) * jax.nn.silu(mixed(old_start))).astype(jnp.bfloat16)
    return (hidden.astype(jnp.float32) + space_mix(blended, w_space)).astype(jnp.bfloat16)
```

```python
import functools

import jax
import jax.numpy as jnp
from jax import lax
from jax.experimental import pallas as pl
from jax.experimental.pallas import tpu as pltpu
from jax.sharding import PartitionSpec as P

PH = 16
PW = 32
OV = 2


epsilon = 1e-06


def passed_along(block, axis, distance):
    devices = range(lax.axis_size(axis))
    route = [(i - distance, i) for i in devices if i - distance in devices]
    return lax.ppermute(block, axis, route)


def rms_norm(array):
    wide = array.astype(jnp.float32)
    return (wide * lax.rsqrt(jnp.mean(wide * wide, axis=-1, keepdims=True) + epsilon)).astype(
        jnp.bfloat16
    )


def project(array, weight):
    extent = array.shape
    product = jnp.dot(array.reshape(-1, extent[-1]), weight, preferred_element_type=jnp.float32)
    return product.reshape(extent[:-1] + (weight.shape[-1],))


def tile_frames(frames, starts):
    reached = starts[None, :] <= frames[:, None]
    new_start = jnp.max(jnp.where(reached, starts[None, :], 0), axis=1)
    earlier = starts[None, :] < new_start[:, None]
    old_start = jnp.max(jnp.where(earlier, starts[None, :], 0), axis=1)
    inside = frames - new_start
    shared = jnp.logical_and(new_start > 0, inside < OV)
    fade = jnp.where(shared, (inside + 1).astype(jnp.float32) / float(OV + 1), jnp.float32(1.0))
    return (new_start, old_start, fade[:, None, None])


def attend(triple):
    queries, key_rows, values = triple
    length = queries.shape[0]
    scale = queries.shape[-1] ** (-0.5)
    scores = (
        jnp.einsum("fipc,gipc->ipfg", queries, key_rows, preferred_element_type=jnp.float32) * scale
    )
    order = jnp.arange(length)
    causal = order[:, None] >= order[None, :]
    scores = jnp.where(causal[None, None], scores, jnp.float32(-1e30))
    peak = jnp.max(scores, axis=-1, keepdims=True)
    expo = jnp.exp(scores - peak)
    weights = (expo / jnp.sum(expo, axis=-1, keepdims=True)).astype(jnp.bfloat16)
    return jnp.einsum(
        "ipfg,gipc->fipc", weights, values, preferred_element_type=jnp.float32
    ).astype(jnp.bfloat16)


def time_blend(padded, frames, starts, w_time):
    length = frames.shape[0]
    extent = padded.shape
    channels = extent[-1]
    flattened = padded.reshape(-1, channels)
    products = [
        jnp.dot(flattened, w_time[lag_index], preferred_element_type=jnp.float32).reshape(
            extent[0], -1, channels
        )
        for lag_index in range(3)
    ]
    new_start, old_start, fade = tile_frames(frames, starts)

    def mixed(context):
        summed = jnp.zeros((length,) + products[0].shape[1:], jnp.float32)
        for lag_index in range(3):
            actual = jnp.minimum(lag_index, frames - context)
            for delta_back in range(lag_index + 1):
                chosen = (actual == delta_back).astype(jnp.float32)[:, None, None]
                summed = (
                    summed + chosen * products[lag_index][2 - delta_back : 2 - delta_back + length]
                )
        return summed

    blended = fade * jax.nn.silu(mixed(new_start)) + (1.0 - fade) * jax.nn.silu(mixed(old_start))
    return blended.astype(jnp.bfloat16)


def space_mix(blended, hidden, w_space):
    length = blended.shape[0]
    channels = blended.shape[-1]
    spatial = blended.reshape(length, PH, PW, channels)
    padded = jnp.pad(spatial, ((0, 0), (1, 1), (1, 1), (0, 0)))
    summed = hidden.reshape(-1, channels).astype(jnp.float32)
    for row_shift in range(3):
        for col_shift in range(3):
            window = padded[:, row_shift : row_shift + PH, col_shift : col_shift + PW].reshape(
                -1, channels
            )
            summed = summed + jnp.dot(
                window, w_space[row_shift, col_shift], preferred_element_type=jnp.float32
            )
    return summed.reshape(length, PH * PW, channels).astype(jnp.bfloat16)


def body(latents, w_query, w_key, w_value, w_out, w_time, w_space, tile_starts):
    frames_dev, row_count, channels = latents.shape
    devices_tm = lax.axis_size("tm")
    share = row_count // devices_tm
    normed = rms_norm(latents).reshape(frames_dev, devices_tm, share, channels)
    queries = project(normed, w_query).astype(jnp.bfloat16)
    key_rows = project(normed, w_key).astype(jnp.bfloat16)
    values = project(normed, w_value).astype(jnp.bfloat16)
    attended = attend(
        (
            lax.all_to_all(queries, "tm", split_axis=1, concat_axis=0, tiled=True),
            lax.all_to_all(key_rows, "tm", split_axis=1, concat_axis=0, tiled=True),
            lax.all_to_all(values, "tm", split_axis=1, concat_axis=0, tiled=True),
        )
    )
    attended = lax.all_to_all(attended, "tm", split_axis=0, concat_axis=1, tiled=True).reshape(
        frames_dev, row_count, channels
    )
    hidden = (latents.astype(jnp.float32) + project(attended, w_out)).astype(jnp.bfloat16)
    smooth = rms_norm(hidden)
    reach = (frames_dev + 1) // frames_dev
    pieces = [passed_along(smooth, "tm", stride) for stride in range(reach, 0, -1)]
    earlier = jnp.concatenate(pieces, axis=0)
    offset = lax.axis_index("tm") * frames_dev
    frames = offset + jnp.arange(frames_dev)
    blended = time_blend(jnp.concatenate([earlier, smooth], axis=0), frames, tile_starts, w_time)
    return space_mix(blended, hidden, w_space)


BS = 4
BLOCK = BS * BS
GROUP = 128


def iota(shape, dim):
    return lax.broadcasted_iota(jnp.int32, shape, dim)


def one_hot(target, columns):
    rows = target.shape[0]
    return (jnp.broadcast_to(target, (rows, columns)) == iota((rows, columns), 1)).astype(
        jnp.float32
    ).astype(jnp.bfloat16)


def matmul(left, right):
    return jnp.dot(left, right, preferred_element_type=jnp.float32)


def place_of(device):
    core, x, y, z = device % 2, (device // 2) % 2, (device // 4) % 2, device // 8
    return 2 * y + (x + y) % 2, 2 * z + core


def device_at(row, column):
    y = row // 2
    return (column // 2) * 8 + y * 4 + ((row % 2 + y) % 2) * 2 + column % 2


def window_position():
    r = iota((PH * PW, 1), 0)
    device, q = r >> 4, r & 15
    core, x, y, z = device & 1, (device >> 1) & 1, (device >> 2) & 1, device >> 3
    row, column = 2 * y + (x ^ y), 2 * z + core
    return (row * BS + (q >> 2)) * PW + column * BS + (q & 3)


def block_position():
    p = iota((PH * PW, 1), 0)
    py, px = p >> 5, p & 31
    row, column = py >> 2, px >> 2
    y = row >> 1
    device = (column >> 1) * 8 + y * 4 + ((row & 1) ^ y) * 2 + (column & 1)
    return device * BLOCK + (py & 3) * BS + (px & 3)


def normalized(wide):
    scale = lax.rsqrt(jnp.mean(wide * wide, axis=-1, keepdims=True) + epsilon)
    return (wide * scale).astype(jnp.bfloat16)


def silu(v):
    return v / (1.0 + jnp.exp(-v))


def block_kernel(
    starts,
    latents,
    wq_any,
    wk_any,
    wv_any,
    wo_any,
    wt_any,
    ws_any,
    out,
    wq,
    wk,
    wv,
    wo,
    wt,
    ws,
    outgoing,
    arrived,
    ext,
    back,
    returned,
    current,
    weight_sem,
    sent,
    got,
    halo_sent,
    halo_got,
    back_sent,
    back_got,
    *,
    n,
):
    frames = n
    channels = latents.shape[-1]
    rows = BLOCK * frames
    me = lax.axis_index("tm")
    mesh_id = pl.DeviceIdType.MESH

    barrier = pltpu.get_barrier_semaphore()

    @pl.loop(1, n)
    def _(k):
        pl.semaphore_signal(
            barrier, inc=1, device_id={"tm": (me + k) % n}, device_id_type=mesh_id
        )

    weights = [
        pltpu.make_async_copy(source, target, weight_sem.at[i])
        for i, (source, target) in enumerate(
            ((wq_any, wq), (wk_any, wk), (wv_any, wv), (wo_any, wo), (wt_any, wt), (ws_any, ws))
        )
    ]
    for copy in weights:
        copy.start()

    outgoing[...] = (
        matmul(one_hot(window_position(), PH * PW), latents[0])
        .astype(jnp.bfloat16)
        .reshape(n, BLOCK, channels)
    )
    pl.semaphore_wait(barrier, n - 1)

    def in_copy(k):
        peer = (me + k) % n
        return pltpu.make_async_remote_copy(
            src_ref=outgoing.at[peer],
            dst_ref=arrived.at[me],
            send_sem=sent.at[k],
            recv_sem=got.at[k],
            device_id={"tm": peer},
            device_id_type=mesh_id,
        )

    @pl.loop(1, n)
    def _(k):
        in_copy(k).start()

    arrived[me] = outgoing[me]

    row, column = place_of(me)
    edge = jnp.zeros((BS + 2, frames, channels), jnp.bfloat16)

    @pl.when(row == 0)
    def _():
        ext[0] = edge

    @pl.when(row == PH // BS - 1)
    def _():
        ext[BS + 1] = edge

    @pl.when(column == 0)
    def _():
        for i in range(BS + 2):
            ext[i, 0] = edge[0]

    @pl.when(column == PW // BS - 1)
    def _():
        for i in range(BS + 2):
            ext[i, BS + 1] = edge[0]

    r = iota((GROUP, 1), 0)
    frame = r % frames
    base = r - frame
    new_start = jnp.zeros((GROUP, 1), jnp.int32)
    for t in range(starts.shape[0]):
        new_start = jnp.maximum(new_start, jnp.where(frame >= starts[t], starts[t], 0))
    old_start = jnp.zeros((GROUP, 1), jnp.int32)
    for t in range(starts.shape[0]):
        old_start = jnp.maximum(old_start, jnp.where(new_start > starts[t], starts[t], 0))
    inside = frame - new_start
    fade = jnp.where(
        jnp.logical_and(new_start > 0, inside < OV),
        (inside + 1).astype(jnp.float32) / float(OV + 1),
        jnp.float32(1.0),
    )
    lags = [
        [one_hot(base + jnp.maximum(frame - j, start), GROUP) for j in (1, 2)]
        for start in (new_start, old_start)
    ]
    other = iota((GROUP, GROUP), 1)
    wide_frame, wide_base = jnp.broadcast_to(frame, other.shape), jnp.broadcast_to(base, other.shape)
    seen = jnp.logical_and(other >= wide_base, other <= wide_base + wide_frame)

    flat = iota((rows, 1), 0)
    by_position = one_hot((flat % frames) * BLOCK + flat // frames, rows)
    by_frame = one_hot((flat % BLOCK) * frames + flat // BLOCK, rows)

    @pl.loop(1, n)
    def _(k):
        in_copy(k).wait_recv()

    held = matmul(by_position, arrived[...].reshape(rows, channels))
    normed = normalized(held)
    for copy in weights[:3]:
        copy.wait()
    queries = matmul(normed, wq[...]).astype(jnp.bfloat16)
    key_rows = matmul(normed, wk[...]).astype(jnp.bfloat16)
    values = matmul(normed, wv[...]).astype(jnp.bfloat16)
    attended = []
    for g in range(rows // GROUP):
        part = slice(g * GROUP, (g + 1) * GROUP)
        scores = lax.dot_general(
            queries[part],
            key_rows[part],
            (((1,), (1,)), ((), ())),
            preferred_element_type=jnp.float32,
        ) * (channels ** (-0.5))
        scores = jnp.where(seen, scores, jnp.float32(-1e30))
        expo = jnp.exp(scores - jnp.max(scores, axis=-1, keepdims=True))
        share = (expo / jnp.sum(expo, axis=-1, keepdims=True)).astype(jnp.bfloat16)
        attended.append(matmul(share, values[part]).astype(jnp.bfloat16))
    weights[3].wait()
    hidden = (held + matmul(jnp.concatenate(attended, axis=0), wo[...])).astype(jnp.bfloat16)
    smooth = normalized(hidden.astype(jnp.float32))

    weights[4].wait()
    current[...] = matmul(smooth, wt[0])
    lag_weights = wt[1:3].reshape(2 * channels, channels)
    mixes = []
    for pair in lags:
        lagged = jnp.concatenate(
            [
                jnp.concatenate(
                    [
                        matmul(lag, smooth[g * GROUP : (g + 1) * GROUP]).astype(jnp.bfloat16)
                        for lag in pair
                    ],
                    axis=1,
                )
                for g in range(rows // GROUP)
            ],
            axis=0,
        )
        mixes.append(current[...] + matmul(lagged, lag_weights))
    fade = jnp.concatenate([fade] * (rows // GROUP), axis=0)
    blended = (fade * silu(mixes[0]) + (1.0 - fade) * silu(mixes[1])).astype(jnp.bfloat16)
    ext[1 : BS + 1, 1 : BS + 1] = blended.reshape(BS, BS, frames, channels)

    def span(step, sending):
        if step == 0:
            return pl.ds(1, BS)
        if sending:
            return pl.ds(1 if step < 0 else BS, 1)
        return pl.ds(BS + 1 if step < 0 else 0, 1)

    halo = []
    for i, (down, right) in enumerate(
        ((-1, 0), (1, 0), (0, -1), (0, 1), (-1, -1), (-1, 1), (1, -1), (1, 1))
    ):
        to_row, to_column = row + down, column + right
        there = jnp.logical_and(
            jnp.logical_and(to_row >= 0, to_row < PH // BS),
            jnp.logical_and(to_column >= 0, to_column < PW // BS),
        )
        from_row, from_column = row - down, column - right
        comes = jnp.logical_and(
            jnp.logical_and(from_row >= 0, from_row < PH // BS),
            jnp.logical_and(from_column >= 0, from_column < PW // BS),
        )
        peer = device_at((to_row + PH // BS) % (PH // BS), (to_column + PW // BS) % (PW // BS))
        copy = pltpu.make_async_remote_copy(
            src_ref=ext.at[span(down, True), span(right, True)],
            dst_ref=ext.at[span(down, False), span(right, False)],
            send_sem=halo_sent.at[i],
            recv_sem=halo_got.at[i],
            device_id={"tm": peer},
            device_id_type=mesh_id,
        )
        halo.append((copy, there, comes))

    for copy, there, comes in halo:

        @pl.when(there)
        def _():
            copy.start()

    weights[5].wait()
    total = hidden.astype(jnp.float32) + matmul(blended, ws[1, 1])

    for copy, there, comes in halo:

        @pl.when(comes)
        def _():
            copy.wait_recv()

    for a in range(3):
        for b in range(3):
            if (a, b) != (1, 1):
                window = ext[a : a + BS, b : b + BS].reshape(rows, channels)
                total = total + matmul(window, ws[a, b])
    decoded = total.astype(jnp.bfloat16)
    back[...] = (
        matmul(by_frame, decoded).astype(jnp.bfloat16).reshape(frames, BLOCK, channels)
    )

    def back_copy(k):
        peer = (me + k) % n
        return pltpu.make_async_remote_copy(
            src_ref=back.at[peer],
            dst_ref=returned.at[me],
            send_sem=back_sent.at[k],
            recv_sem=back_got.at[k],
            device_id={"tm": peer},
            device_id_type=mesh_id,
        )

    @pl.loop(1, n)
    def _(k):
        back_copy(k).start()

    returned[me] = back[me]
    to_window = one_hot(block_position(), PH * PW)

    @pl.loop(1, n)
    def _(k):
        in_copy(k).wait_send()

    for copy, there, comes in halo:

        @pl.when(there)
        def _():
            copy.wait_send()

    @pl.loop(1, n)
    def _(k):
        back_copy(k).wait_recv()

    out[0] = matmul(to_window, returned[...].reshape(PH * PW, channels)).astype(jnp.bfloat16)

    @pl.loop(1, n)
    def _(k):
        back_copy(k).wait_send()


def block_body(latents, w_query, w_key, w_value, w_out, w_time, w_space, tile_starts):
    n = lax.axis_size("tm")
    channels = latents.shape[-1]
    vmem = pl.BlockSpec(memory_space=pltpu.VMEM)
    anywhere = pl.BlockSpec(memory_space=pl.ANY)
    dma = pltpu.SemaphoreType.DMA
    bf16 = jnp.bfloat16
    return pl.pallas_call(
        functools.partial(block_kernel, n=n),
        out_shape=jax.ShapeDtypeStruct(latents.shape, bf16),
        in_specs=[pl.BlockSpec(memory_space=pltpu.SMEM), vmem] + [anywhere] * 6,
        out_specs=vmem,
        scratch_shapes=[
            pltpu.VMEM(w_query.shape, bf16),
            pltpu.VMEM(w_key.shape, bf16),
            pltpu.VMEM(w_value.shape, bf16),
            pltpu.VMEM(w_out.shape, bf16),
            pltpu.VMEM(w_time.shape, bf16),
            pltpu.VMEM(w_space.shape, bf16),
            pltpu.VMEM((n, BLOCK, channels), bf16),
            pltpu.VMEM((n, BLOCK, channels), bf16),
            pltpu.VMEM((BS + 2, BS + 2, n, channels), bf16),
            pltpu.VMEM((n, BLOCK, channels), bf16),
            pltpu.VMEM((n, BLOCK, channels), bf16),
            pltpu.VMEM((n * BLOCK, channels), jnp.float32),
            dma((6,)),
            dma((n,)),
            dma((n,)),
            dma((8,)),
            dma((8,)),
            dma((n,)),
            dma((n,)),
        ],
        compiler_params=pltpu.CompilerParams(
            collective_id=0, has_side_effects=True, vmem_limit_bytes=48 * 2**20
        ),
    )(tile_starts, latents, w_query, w_key, w_value, w_out, w_time, w_space)


def any_body(latents, *rest):
    frames_dev, row_count, channels = latents.shape
    blocks = (PH // BS) * (PW // BS)
    if frames_dev == 1 and lax.axis_size("tm") == blocks and row_count == PH * PW:
        return block_body(latents, *rest)
    return body(latents, *rest)


def solution(mesh):
    placed = (P(("groups", "tm"), None, None), P(), P(), P(), P(), P(), P(), P("groups"))
    return jax.shard_map(
        any_body, mesh=mesh, in_specs=placed, out_specs=P(("groups", "tm"), None, None), check_vma=False
    )
```

```python
import functools

import jax
import jax.numpy as jnp
from jax import lax
from jax.experimental import pallas as pl
from jax.experimental.pallas import tpu as pltpu
from jax.sharding import PartitionSpec as P

PH = 16
PW = 32
OV = 2


epsilon = 1e-06


def passed_along(block, axis, distance):
    devices = range(lax.axis_size(axis))
    route = [(i - distance, i) for i in devices if i - distance in devices]
    return lax.ppermute(block, axis, route)


def rms_norm(array):
    wide = array.astype(jnp.float32)
    return (wide * lax.rsqrt(jnp.mean(wide * wide, axis=-1, keepdims=True) + epsilon)).astype(
        jnp.bfloat16
    )


def project(array, weight):
    extent = array.shape
    product = jnp.dot(array.reshape(-1, extent[-1]), weight, preferred_element_type=jnp.float32)
    return product.reshape(extent[:-1] + (weight.shape[-1],))


def tile_frames(frames, starts):
    reached = starts[None, :] <= frames[:, None]
    new_start = jnp.max(jnp.where(reached, starts[None, :], 0), axis=1)
    earlier = starts[None, :] < new_start[:, None]
    old_start = jnp.max(jnp.where(earlier, starts[None, :], 0), axis=1)
    inside = frames - new_start
    shared = jnp.logical_and(new_start > 0, inside < OV)
    fade = jnp.where(shared, (inside + 1).astype(jnp.float32) / float(OV + 1), jnp.float32(1.0))
    return (new_start, old_start, fade[:, None, None])


def attend(triple):
    queries, key_rows, values = triple
    length = queries.shape[0]
    scale = queries.shape[-1] ** (-0.5)
    scores = (
        jnp.einsum("fipc,gipc->ipfg", queries, key_rows, preferred_element_type=jnp.float32) * scale
    )
    order = jnp.arange(length)
    causal = order[:, None] >= order[None, :]
    scores = jnp.where(causal[None, None], scores, jnp.float32(-1e30))
    peak = jnp.max(scores, axis=-1, keepdims=True)
    expo = jnp.exp(scores - peak)
    weights = (expo / jnp.sum(expo, axis=-1, keepdims=True)).astype(jnp.bfloat16)
    return jnp.einsum(
        "ipfg,gipc->fipc", weights, values, preferred_element_type=jnp.float32
    ).astype(jnp.bfloat16)


def time_blend(padded, frames, starts, w_time):
    length = frames.shape[0]
    extent = padded.shape
    channels = extent[-1]
    flattened = padded.reshape(-1, channels)
    products = [
        jnp.dot(flattened, w_time[lag_index], preferred_element_type=jnp.float32).reshape(
            extent[0], -1, channels
        )
        for lag_index in range(3)
    ]
    new_start, old_start, fade = tile_frames(frames, starts)

    def mixed(context):
        summed = jnp.zeros((length,) + products[0].shape[1:], jnp.float32)
        for lag_index in range(3):
            actual = jnp.minimum(lag_index, frames - context)
            for delta_back in range(lag_index + 1):
                chosen = (actual == delta_back).astype(jnp.float32)[:, None, None]
                summed = (
                    summed + chosen * products[lag_index][2 - delta_back : 2 - delta_back + length]
                )
        return summed

    blended = fade * jax.nn.silu(mixed(new_start)) + (1.0 - fade) * jax.nn.silu(mixed(old_start))
    return blended.astype(jnp.bfloat16)


def space_mix(blended, hidden, w_space):
    length = blended.shape[0]
    channels = blended.shape[-1]
    spatial = blended.reshape(length, PH, PW, channels)
    padded = jnp.pad(spatial, ((0, 0), (1, 1), (1, 1), (0, 0)))
    summed = hidden.reshape(-1, channels).astype(jnp.float32)
    for row_shift in range(3):
        for col_shift in range(3):
            window = padded[:, row_shift : row_shift + PH, col_shift : col_shift + PW].reshape(
                -1, channels
            )
            summed = summed + jnp.dot(
                window, w_space[row_shift, col_shift], preferred_element_type=jnp.float32
            )
    return summed.reshape(length, PH * PW, channels).astype(jnp.bfloat16)


def body(latents, w_query, w_key, w_value, w_out, w_time, w_space, tile_starts):
    frames_dev, row_count, channels = latents.shape
    devices_tm = lax.axis_size("tm")
    share = row_count // devices_tm
    normed = rms_norm(latents).reshape(frames_dev, devices_tm, share, channels)
    queries = project(normed, w_query).astype(jnp.bfloat16)
    key_rows = project(normed, w_key).astype(jnp.bfloat16)
    values = project(normed, w_value).astype(jnp.bfloat16)
    attended = attend(
        (
            lax.all_to_all(queries, "tm", split_axis=1, concat_axis=0, tiled=True),
            lax.all_to_all(key_rows, "tm", split_axis=1, concat_axis=0, tiled=True),
            lax.all_to_all(values, "tm", split_axis=1, concat_axis=0, tiled=True),
        )
    )
    attended = lax.all_to_all(attended, "tm", split_axis=0, concat_axis=1, tiled=True).reshape(
        frames_dev, row_count, channels
    )
    hidden = (latents.astype(jnp.float32) + project(attended, w_out)).astype(jnp.bfloat16)
    smooth = rms_norm(hidden)
    reach = (frames_dev + 1) // frames_dev
    pieces = [passed_along(smooth, "tm", stride) for stride in range(reach, 0, -1)]
    earlier = jnp.concatenate(pieces, axis=0)
    offset = lax.axis_index("tm") * frames_dev
    frames = offset + jnp.arange(frames_dev)
    blended = time_blend(jnp.concatenate([earlier, smooth], axis=0), frames, tile_starts, w_time)
    return space_mix(blended, hidden, w_space)


BS = 4
BLOCK = BS * BS
GROUP = 128


def iota(shape, dim):
    return lax.broadcasted_iota(jnp.int32, shape, dim)


def one_hot(target, columns):
    rows = target.shape[0]
    return (jnp.broadcast_to(target, (rows, columns)) == iota((rows, columns), 1)).astype(
        jnp.float32
    ).astype(jnp.bfloat16)


def matmul(left, right):
    return jnp.dot(left, right, preferred_element_type=jnp.float32)


def place_of(device):
    core, x, y, z = device % 2, (device // 2) % 2, (device // 4) % 2, device // 8
    return 2 * y + (x + y) % 2, 2 * z + core


def device_at(row, column):
    y = row // 2
    return (column // 2) * 8 + y * 4 + ((row % 2 + y) % 2) * 2 + column % 2


def window_position():
    r = iota((PH * PW, 1), 0)
    device, q = r >> 4, r & 15
    core, x, y, z = device & 1, (device >> 1) & 1, (device >> 2) & 1, device >> 3
    row, column = 2 * y + (x ^ y), 2 * z + core
    return (row * BS + (q >> 2)) * PW + column * BS + (q & 3)


def block_position():
    p = iota((PH * PW, 1), 0)
    py, px = p >> 5, p & 31
    row, column = py >> 2, px >> 2
    y = row >> 1
    device = (column >> 1) * 8 + y * 4 + ((row & 1) ^ y) * 2 + (column & 1)
    return device * BLOCK + (py & 3) * BS + (px & 3)


def normalized(wide):
    scale = lax.rsqrt(jnp.mean(wide * wide, axis=-1, keepdims=True) + epsilon)
    return (wide * scale).astype(jnp.bfloat16)


def silu(v):
    return v / (1.0 + jnp.exp(-v))


def block_kernel(
    starts,
    latents,
    wq_any,
    wk_any,
    wv_any,
    wo_any,
    wt_any,
    ws_any,
    out,
    wq,
    wk,
    wv,
    wo,
    wt,
    ws,
    outgoing,
    arrived,
    ext,
    back,
    returned,
    current,
    weight_sem,
    sent,
    got,
    halo_sent,
    halo_got,
    back_sent,
    back_got,
    *,
    n,
):
    frames = n
    channels = latents.shape[-1]
    rows = BLOCK * frames
    me = lax.axis_index("tm")
    mesh_id = pl.DeviceIdType.MESH

    barrier = pltpu.get_barrier_semaphore()

    @pl.loop(1, n)
    def _(k):
        pl.semaphore_signal(
            barrier, inc=1, device_id={"tm": (me + k) % n}, device_id_type=mesh_id
        )

    weights = [
        pltpu.make_async_copy(source, target, weight_sem.at[i])
        for i, (source, target) in enumerate(
            ((wq_any, wq), (wk_any, wk), (wv_any, wv), (wo_any, wo), (wt_any, wt), (ws_any, ws))
        )
    ]
    for copy in weights:
        copy.start()

    outgoing[...] = (
        matmul(one_hot(window_position(), PH * PW), latents[0])
        .astype(jnp.bfloat16)
        .reshape(n, BLOCK, channels)
    )
    pl.semaphore_wait(barrier, n - 1)

    def in_copy(k):
        peer = (me + k) % n
        return pltpu.make_async_remote_copy(
            src_ref=outgoing.at[peer],
            dst_ref=arrived.at[me],
            send_sem=sent.at[k],
            recv_sem=got.at[k],
            device_id={"tm": peer},
            device_id_type=mesh_id,
        )

    @pl.loop(1, n)
    def _(k):
        in_copy(k).start()

    arrived[me] = outgoing[me]

    row, column = place_of(me)
    edge = jnp.zeros((BS + 2, frames, channels), jnp.bfloat16)

    @pl.when(row == 0)
    def _():
        ext[0] = edge

    @pl.when(row == PH // BS - 1)
    def _():
        ext[BS + 1] = edge

    @pl.when(column == 0)
    def _():
        for i in range(BS + 2):
            ext[i, 0] = edge[0]

    @pl.when(column == PW // BS - 1)
    def _():
        for i in range(BS + 2):
            ext[i, BS + 1] = edge[0]

    r = iota((GROUP, 1), 0)
    frame = r % frames
    base = r - frame
    new_start = jnp.zeros((GROUP, 1), jnp.int32)
    for t in range(starts.shape[0]):
        new_start = jnp.maximum(new_start, jnp.where(frame >= starts[t], starts[t], 0))
    old_start = jnp.zeros((GROUP, 1), jnp.int32)
    for t in range(starts.shape[0]):
        old_start = jnp.maximum(old_start, jnp.where(new_start > starts[t], starts[t], 0))
    inside = frame - new_start
    fade = jnp.where(
        jnp.logical_and(new_start > 0, inside < OV),
        (inside + 1).astype(jnp.float32) / float(OV + 1),
        jnp.float32(1.0),
    )
    lags = [
        [one_hot(base + jnp.maximum(frame - j, start), GROUP) for j in (1, 2)]
        for start in (new_start, old_start)
    ]
    other = iota((GROUP, GROUP), 1)
    wide_frame, wide_base = jnp.broadcast_to(frame, other.shape), jnp.broadcast_to(base, other.shape)
    seen = jnp.logical_and(other >= wide_base, other <= wide_base + wide_frame)

    flat = iota((rows, 1), 0)
    by_position = one_hot((flat % frames) * BLOCK + flat // frames, rows)
    by_frame = one_hot((flat % BLOCK) * frames + flat // BLOCK, rows)

    @pl.loop(1, n)
    def _(k):
        in_copy(k).wait_recv()

    held = matmul(by_position, arrived[...].reshape(rows, channels))
    normed = normalized(held)
    for copy in weights[:3]:
        copy.wait()
    queries = matmul(normed, wq[...]).astype(jnp.bfloat16)
    key_rows = matmul(normed, wk[...]).astype(jnp.bfloat16)
    values = matmul(normed, wv[...]).astype(jnp.bfloat16)
    attended = []
    for g in range(rows // GROUP):
        part = slice(g * GROUP, (g + 1) * GROUP)
        scores = lax.dot_general(
            queries[part],
            key_rows[part],
            (((1,), (1,)), ((), ())),
            preferred_element_type=jnp.float32,
        ) * (channels ** (-0.5))
        scores = jnp.where(seen, scores, jnp.float32(-1e30))
        expo = jnp.exp(scores - jnp.max(scores, axis=-1, keepdims=True))
        share = (expo / jnp.sum(expo, axis=-1, keepdims=True)).astype(jnp.bfloat16)
        attended.append(matmul(share, values[part]).astype(jnp.bfloat16))
    weights[3].wait()
    hidden = (held + matmul(jnp.concatenate(attended, axis=0), wo[...])).astype(jnp.bfloat16)
    smooth = normalized(hidden.astype(jnp.float32))

    weights[4].wait()
    current[...] = matmul(smooth, wt[0])
    lag_weights = wt[1:3].reshape(2 * channels, channels)
    mixes = []
    for pair in lags:
        lagged = jnp.concatenate(
            [
                jnp.concatenate(
                    [
                        matmul(lag, smooth[g * GROUP : (g + 1) * GROUP]).astype(jnp.bfloat16)
                        for lag in pair
                    ],
                    axis=1,
                )
                for g in range(rows // GROUP)
            ],
            axis=0,
        )
        mixes.append(current[...] + matmul(lagged, lag_weights))
    fade = jnp.concatenate([fade] * (rows // GROUP), axis=0)
    blended = (fade * silu(mixes[0]) + (1.0 - fade) * silu(mixes[1])).astype(jnp.bfloat16)
    ext[1 : BS + 1, 1 : BS + 1] = blended.reshape(BS, BS, frames, channels)

    def span(step, sending):
        if step == 0:
            return pl.ds(1, BS)
        if sending:
            return pl.ds(1 if step < 0 else BS, 1)
        return pl.ds(BS + 1 if step < 0 else 0, 1)

    halo = []
    for i, (down, right) in enumerate(
        ((-1, 0), (1, 0), (0, -1), (0, 1), (-1, -1), (-1, 1), (1, -1), (1, 1))
    ):
        to_row, to_column = row + down, column + right
        there = jnp.logical_and(
            jnp.logical_and(to_row >= 0, to_row < PH // BS),
            jnp.logical_and(to_column >= 0, to_column < PW // BS),
        )
        from_row, from_column = row - down, column - right
        comes = jnp.logical_and(
            jnp.logical_and(from_row >= 0, from_row < PH // BS),
            jnp.logical_and(from_column >= 0, from_column < PW // BS),
        )
        peer = device_at((to_row + PH // BS) % (PH // BS), (to_column + PW // BS) % (PW // BS))
        copy = pltpu.make_async_remote_copy(
            src_ref=ext.at[span(down, True), span(right, True)],
            dst_ref=ext.at[span(down, False), span(right, False)],
            send_sem=halo_sent.at[i],
            recv_sem=halo_got.at[i],
            device_id={"tm": peer},
            device_id_type=mesh_id,
        )
        halo.append((copy, there, comes))

    for copy, there, comes in halo:

        @pl.when(there)
        def _():
            copy.start()

    weights[5].wait()
    current[...] = hidden.astype(jnp.float32) + matmul(blended, ws[1, 1])

    for copy, there, comes in halo:

        @pl.when(comes)
        def _():
            copy.wait_recv()

    half = channels // 2

    def back_copy(k, h):
        peer = (me + k) % n
        return pltpu.make_async_remote_copy(
            src_ref=back.at[h, peer],
            dst_ref=returned.at[h, me],
            send_sem=back_sent.at[h, k],
            recv_sem=back_got.at[h, k],
            device_id={"tm": peer},
            device_id_type=mesh_id,
        )

    for h in range(2):
        part = slice(h * half, (h + 1) * half)
        total = current[:, part]
        for a in range(3):
            for b in range(3):
                if (a, b) != (1, 1):
                    window = ext[a : a + BS, b : b + BS].reshape(rows, channels)
                    total = total + matmul(window, ws[a, b, :, part])
        back[h] = (
            matmul(by_frame, total.astype(jnp.bfloat16))
            .astype(jnp.bfloat16)
            .reshape(frames, BLOCK, half)
        )

        @pl.loop(1, n)
        def _(k):
            back_copy(k, h).start()

        returned[h, me] = back[h, me]

    to_window = one_hot(block_position(), PH * PW)

    @pl.loop(1, n)
    def _(k):
        in_copy(k).wait_send()

    for copy, there, comes in halo:

        @pl.when(there)
        def _():
            copy.wait_send()

    for h in range(2):

        @pl.loop(1, n)
        def _(k):
            back_copy(k, h).wait_recv()

        out[0, :, h * half : (h + 1) * half] = matmul(
            to_window, returned[h].reshape(PH * PW, half)
        ).astype(jnp.bfloat16)

    for h in range(2):

        @pl.loop(1, n)
        def _(k):
            back_copy(k, h).wait_send()


def block_body(latents, w_query, w_key, w_value, w_out, w_time, w_space, tile_starts):
    n = lax.axis_size("tm")
    channels = latents.shape[-1]
    vmem = pl.BlockSpec(memory_space=pltpu.VMEM)
    anywhere = pl.BlockSpec(memory_space=pltpu.HBM)
    dma = pltpu.SemaphoreType.DMA
    bf16 = jnp.bfloat16
    return pl.pallas_call(
        functools.partial(block_kernel, n=n),
        out_shape=jax.ShapeDtypeStruct(latents.shape, bf16),
        in_specs=[pl.BlockSpec(memory_space=pltpu.SMEM), vmem] + [anywhere] * 6,
        out_specs=vmem,
        scratch_shapes=[
            pltpu.VMEM(w_query.shape, bf16),
            pltpu.VMEM(w_key.shape, bf16),
            pltpu.VMEM(w_value.shape, bf16),
            pltpu.VMEM(w_out.shape, bf16),
            pltpu.VMEM(w_time.shape, bf16),
            pltpu.VMEM(w_space.shape, bf16),
            pltpu.VMEM((n, BLOCK, channels), bf16),
            pltpu.VMEM((n, BLOCK, channels), bf16),
            pltpu.VMEM((BS + 2, BS + 2, n, channels), bf16),
            pltpu.VMEM((2, n, BLOCK, channels // 2), bf16),
            pltpu.VMEM((2, n, BLOCK, channels // 2), bf16),
            pltpu.VMEM((n * BLOCK, channels), jnp.float32),
            dma((6,)),
            dma((n,)),
            dma((n,)),
            dma((8,)),
            dma((8,)),
            dma((2, n)),
            dma((2, n)),
        ],
        compiler_params=pltpu.CompilerParams(
            collective_id=0, has_side_effects=True, vmem_limit_bytes=60 * 2**20
        ),
    )(tile_starts, latents, w_query, w_key, w_value, w_out, w_time, w_space)


def any_body(latents, *rest):
    frames_dev, row_count, channels = latents.shape
    blocks = (PH // BS) * (PW // BS)
    if frames_dev == 1 and lax.axis_size("tm") == blocks and row_count == PH * PW:
        return block_body(latents, *rest)
    return body(latents, *rest)


def solution(mesh):
    placed = (P(("groups", "tm"), None, None), P(), P(), P(), P(), P(), P(), P("groups"))
    return jax.shard_map(
        any_body, mesh=mesh, in_specs=placed, out_specs=P(("groups", "tm"), None, None), check_vma=False
    )
```

```python
import functools

import jax
import jax.numpy as jnp
from jax import lax
from jax.experimental import pallas as pl
from jax.experimental.pallas import tpu as pltpu
from jax.sharding import PartitionSpec as P

PH = 16
PW = 32
OV = 2


epsilon = 1e-06


def passed_along(block, axis, distance):
    devices = range(lax.axis_size(axis))
    route = [(i - distance, i) for i in devices if i - distance in devices]
    return lax.ppermute(block, axis, route)


def rms_norm(array):
    wide = array.astype(jnp.float32)
    return (wide * lax.rsqrt(jnp.mean(wide * wide, axis=-1, keepdims=True) + epsilon)).astype(
        jnp.bfloat16
    )


def project(array, weight):
    extent = array.shape
    product = jnp.dot(array.reshape(-1, extent[-1]), weight, preferred_element_type=jnp.float32)
    return product.reshape(extent[:-1] + (weight.shape[-1],))


def tile_frames(frames, starts):
    reached = starts[None, :] <= frames[:, None]
    new_start = jnp.max(jnp.where(reached, starts[None, :], 0), axis=1)
    earlier = starts[None, :] < new_start[:, None]
    old_start = jnp.max(jnp.where(earlier, starts[None, :], 0), axis=1)
    inside = frames - new_start
    shared = jnp.logical_and(new_start > 0, inside < OV)
    fade = jnp.where(shared, (inside + 1).astype(jnp.float32) / float(OV + 1), jnp.float32(1.0))
    return (new_start, old_start, fade[:, None, None])


def attend(triple):
    queries, key_rows, values = triple
    length = queries.shape[0]
    scale = queries.shape[-1] ** (-0.5)
    scores = (
        jnp.einsum("fipc,gipc->ipfg", queries, key_rows, preferred_element_type=jnp.float32) * scale
    )
    order = jnp.arange(length)
    causal = order[:, None] >= order[None, :]
    scores = jnp.where(causal[None, None], scores, jnp.float32(-1e30))
    peak = jnp.max(scores, axis=-1, keepdims=True)
    expo = jnp.exp(scores - peak)
    weights = (expo / jnp.sum(expo, axis=-1, keepdims=True)).astype(jnp.bfloat16)
    return jnp.einsum(
        "ipfg,gipc->fipc", weights, values, preferred_element_type=jnp.float32
    ).astype(jnp.bfloat16)


def time_blend(padded, frames, starts, w_time):
    length = frames.shape[0]
    extent = padded.shape
    channels = extent[-1]
    flattened = padded.reshape(-1, channels)
    products = [
        jnp.dot(flattened, w_time[lag_index], preferred_element_type=jnp.float32).reshape(
            extent[0], -1, channels
        )
        for lag_index in range(3)
    ]
    new_start, old_start, fade = tile_frames(frames, starts)

    def mixed(context):
        summed = jnp.zeros((length,) + products[0].shape[1:], jnp.float32)
        for lag_index in range(3):
            actual = jnp.minimum(lag_index, frames - context)
            for delta_back in range(lag_index + 1):
                chosen = (actual == delta_back).astype(jnp.float32)[:, None, None]
                summed = (
                    summed + chosen * products[lag_index][2 - delta_back : 2 - delta_back + length]
                )
        return summed

    blended = fade * jax.nn.silu(mixed(new_start)) + (1.0 - fade) * jax.nn.silu(mixed(old_start))
    return blended.astype(jnp.bfloat16)


def space_mix(blended, hidden, w_space):
    length = blended.shape[0]
    channels = blended.shape[-1]
    spatial = blended.reshape(length, PH, PW, channels)
    padded = jnp.pad(spatial, ((0, 0), (1, 1), (1, 1), (0, 0)))
    summed = hidden.reshape(-1, channels).astype(jnp.float32)
    for row_shift in range(3):
        for col_shift in range(3):
            window = padded[:, row_shift : row_shift + PH, col_shift : col_shift + PW].reshape(
                -1, channels
            )
            summed = summed + jnp.dot(
                window, w_space[row_shift, col_shift], preferred_element_type=jnp.float32
            )
    return summed.reshape(length, PH * PW, channels).astype(jnp.bfloat16)


def body(latents, w_query, w_key, w_value, w_out, w_time, w_space, tile_starts):
    frames_dev, row_count, channels = latents.shape
    devices_tm = lax.axis_size("tm")
    share = row_count // devices_tm
    normed = rms_norm(latents).reshape(frames_dev, devices_tm, share, channels)
    queries = project(normed, w_query).astype(jnp.bfloat16)
    key_rows = project(normed, w_key).astype(jnp.bfloat16)
    values = project(normed, w_value).astype(jnp.bfloat16)
    attended = attend(
        (
            lax.all_to_all(queries, "tm", split_axis=1, concat_axis=0, tiled=True),
            lax.all_to_all(key_rows, "tm", split_axis=1, concat_axis=0, tiled=True),
            lax.all_to_all(values, "tm", split_axis=1, concat_axis=0, tiled=True),
        )
    )
    attended = lax.all_to_all(attended, "tm", split_axis=0, concat_axis=1, tiled=True).reshape(
        frames_dev, row_count, channels
    )
    hidden = (latents.astype(jnp.float32) + project(attended, w_out)).astype(jnp.bfloat16)
    smooth = rms_norm(hidden)
    reach = (frames_dev + 1) // frames_dev
    pieces = [passed_along(smooth, "tm", stride) for stride in range(reach, 0, -1)]
    earlier = jnp.concatenate(pieces, axis=0)
    offset = lax.axis_index("tm") * frames_dev
    frames = offset + jnp.arange(frames_dev)
    blended = time_blend(jnp.concatenate([earlier, smooth], axis=0), frames, tile_starts, w_time)
    return space_mix(blended, hidden, w_space)


BS = 4
BLOCK = BS * BS
GROUP = 128


def iota(shape, dim):
    return lax.broadcasted_iota(jnp.int32, shape, dim)


def one_hot(target, columns):
    rows = target.shape[0]
    return (jnp.broadcast_to(target, (rows, columns)) == iota((rows, columns), 1)).astype(
        jnp.float32
    ).astype(jnp.bfloat16)


def matmul(left, right):
    return jnp.dot(left, right, preferred_element_type=jnp.float32)


def place_of(device):
    core, x, y, z = device % 2, (device // 2) % 2, (device // 4) % 2, device // 8
    return 2 * y + (x + y) % 2, 2 * z + core


def device_at(row, column):
    y = row // 2
    return (column // 2) * 8 + y * 4 + ((row % 2 + y) % 2) * 2 + column % 2


def window_position():
    r = iota((PH * PW, 1), 0)
    device, q = r >> 4, r & 15
    core, x, y, z = device & 1, (device >> 1) & 1, (device >> 2) & 1, device >> 3
    row, column = 2 * y + (x ^ y), 2 * z + core
    return (row * BS + (q >> 2)) * PW + column * BS + (q & 3)


def block_position():
    p = iota((PH * PW, 1), 0)
    py, px = p >> 5, p & 31
    row, column = py >> 2, px >> 2
    y = row >> 1
    device = (column >> 1) * 8 + y * 4 + ((row & 1) ^ y) * 2 + (column & 1)
    return device * BLOCK + (py & 3) * BS + (px & 3)


def normalized(wide):
    scale = lax.rsqrt(jnp.mean(wide * wide, axis=-1, keepdims=True) + epsilon)
    return (wide * scale).astype(jnp.bfloat16)


def silu(v):
    return v / (1.0 + jnp.exp(-v))


def block_kernel(
    starts,
    latents,
    wq_any,
    wk_any,
    wv_any,
    wo_any,
    wt_any,
    ws_any,
    out,
    wq,
    wk,
    wv,
    wo,
    wt,
    ws,
    outgoing,
    arrived,
    ext,
    back,
    returned,
    current,
    weight_sem,
    sent,
    got,
    halo_sent,
    halo_got,
    back_sent,
    back_got,
    *,
    n,
):
    frames = n
    channels = latents.shape[-1]
    rows = BLOCK * frames
    me = lax.axis_index("tm")
    mesh_id = pl.DeviceIdType.MESH

    barrier = pltpu.get_barrier_semaphore()

    @pl.loop(1, n)
    def _(k):
        pl.semaphore_signal(
            barrier, inc=1, device_id={"tm": (me + k) % n}, device_id_type=mesh_id
        )

    weights = [
        pltpu.make_async_copy(source, target, weight_sem.at[i])
        for i, (source, target) in enumerate(
            ((wq_any, wq), (wk_any, wk), (wv_any, wv), (wo_any, wo), (wt_any, wt), (ws_any, ws))
        )
    ]
    for copy in weights:
        copy.start()

    outgoing[...] = (
        matmul(one_hot(window_position(), PH * PW), latents[0])
        .astype(jnp.bfloat16)
        .reshape(n, BLOCK, channels)
    )
    pl.semaphore_wait(barrier, n - 1)

    def in_copy(k):
        peer = (me + k) % n
        return pltpu.make_async_remote_copy(
            src_ref=outgoing.at[peer],
            dst_ref=arrived.at[me],
            send_sem=sent.at[k],
            recv_sem=got.at[k],
            device_id={"tm": peer},
            device_id_type=mesh_id,
        )

    @pl.loop(1, n)
    def _(k):
        in_copy(k).start()

    arrived[me] = outgoing[me]

    row, column = place_of(me)
    edge = jnp.zeros((BS + 2, frames, channels), jnp.bfloat16)

    @pl.when(row == 0)
    def _():
        ext[0] = edge

    @pl.when(row == PH // BS - 1)
    def _():
        ext[BS + 1] = edge

    @pl.when(column == 0)
    def _():
        for i in range(BS + 2):
            ext[i, 0] = edge[0]

    @pl.when(column == PW // BS - 1)
    def _():
        for i in range(BS + 2):
            ext[i, BS + 1] = edge[0]

    r = iota((GROUP, 1), 0)
    frame = r % frames
    base = r - frame
    new_start = jnp.zeros((GROUP, 1), jnp.int32)
    for t in range(starts.shape[0]):
        new_start = jnp.maximum(new_start, jnp.where(frame >= starts[t], starts[t], 0))
    old_start = jnp.zeros((GROUP, 1), jnp.int32)
    for t in range(starts.shape[0]):
        old_start = jnp.maximum(old_start, jnp.where(new_start > starts[t], starts[t], 0))
    inside = frame - new_start
    fade = jnp.where(
        jnp.logical_and(new_start > 0, inside < OV),
        (inside + 1).astype(jnp.float32) / float(OV + 1),
        jnp.float32(1.0),
    )
    lags = [
        [one_hot(base + jnp.maximum(frame - j, start), GROUP) for j in (1, 2)]
        for start in (new_start, old_start)
    ]
    other = iota((GROUP, GROUP), 1)
    wide_frame, wide_base = jnp.broadcast_to(frame, other.shape), jnp.broadcast_to(base, other.shape)
    seen = jnp.logical_and(other >= wide_base, other <= wide_base + wide_frame)

    flat = iota((rows, 1), 0)
    by_position = one_hot((flat % frames) * BLOCK + flat // frames, rows)
    by_frame = one_hot((flat % BLOCK) * frames + flat // BLOCK, rows)

    @pl.loop(1, n)
    def _(k):
        in_copy(k).wait_recv()

    held = matmul(by_position, arrived[...].reshape(rows, channels))
    normed = normalized(held)
    for copy in weights[:3]:
        copy.wait()
    queries = matmul(normed, wq[...]).astype(jnp.bfloat16)
    key_rows = matmul(normed, wk[...]).astype(jnp.bfloat16)
    values = matmul(normed, wv[...]).astype(jnp.bfloat16)
    attended = []
    for g in range(rows // GROUP):
        part = slice(g * GROUP, (g + 1) * GROUP)
        scores = lax.dot_general(
            queries[part],
            key_rows[part],
            (((1,), (1,)), ((), ())),
            preferred_element_type=jnp.float32,
        ) * (channels ** (-0.5))
        scores = jnp.where(seen, scores, jnp.float32(-1e30))
        expo = jnp.exp(scores - jnp.max(scores, axis=-1, keepdims=True))
        share = (expo / jnp.sum(expo, axis=-1, keepdims=True)).astype(jnp.bfloat16)
        attended.append(matmul(share, values[part]).astype(jnp.bfloat16))
    weights[3].wait()
    hidden = (held + matmul(jnp.concatenate(attended, axis=0), wo[...])).astype(jnp.bfloat16)
    smooth = normalized(hidden.astype(jnp.float32))

    weights[4].wait()
    current[...] = matmul(smooth, wt[0])
    lag_weights = wt[1:3].reshape(2 * channels, channels)
    mixes = []
    for pair in lags:
        lagged = jnp.concatenate(
            [
                jnp.concatenate(
                    [
                        matmul(lag, smooth[g * GROUP : (g + 1) * GROUP]).astype(jnp.bfloat16)
                        for lag in pair
                    ],
                    axis=1,
                )
                for g in range(rows // GROUP)
            ],
            axis=0,
        )
        mixes.append(current[...] + matmul(lagged, lag_weights))
    fade = jnp.concatenate([fade] * (rows // GROUP), axis=0)
    blended = (fade * silu(mixes[0]) + (1.0 - fade) * silu(mixes[1])).astype(jnp.bfloat16)
    ext[1 : BS + 1, 1 : BS + 1] = blended.reshape(BS, BS, frames, channels)

    def span(step, sending):
        if step == 0:
            return pl.ds(1, BS)
        if sending:
            return pl.ds(1 if step < 0 else BS, 1)
        return pl.ds(BS + 1 if step < 0 else 0, 1)

    halo = []
    for i, (down, right) in enumerate(
        ((-1, 0), (1, 0), (0, -1), (0, 1), (-1, -1), (-1, 1), (1, -1), (1, 1))
    ):
        to_row, to_column = row + down, column + right
        there = jnp.logical_and(
            jnp.logical_and(to_row >= 0, to_row < PH // BS),
            jnp.logical_and(to_column >= 0, to_column < PW // BS),
        )
        from_row, from_column = row - down, column - right
        comes = jnp.logical_and(
            jnp.logical_and(from_row >= 0, from_row < PH // BS),
            jnp.logical_and(from_column >= 0, from_column < PW // BS),
        )
        peer = device_at((to_row + PH // BS) % (PH // BS), (to_column + PW // BS) % (PW // BS))
        copy = pltpu.make_async_remote_copy(
            src_ref=ext.at[span(down, True), span(right, True)],
            dst_ref=ext.at[span(down, False), span(right, False)],
            send_sem=halo_sent.at[i],
            recv_sem=halo_got.at[i],
            device_id={"tm": peer},
            device_id_type=mesh_id,
        )
        halo.append((copy, there, comes))

    for copy, there, comes in halo:

        @pl.when(there)
        def _():
            copy.start()

    weights[5].wait()
    current[...] = hidden.astype(jnp.float32) + matmul(blended, ws[1, 1])

    def arrive(chosen):
        for copy, there, comes in chosen:

            @pl.when(comes)
            def _():
                copy.wait_recv()

    arrive(halo[2:4])
    total = current[...]
    for b in (0, 2):
        window = ext[1 : BS + 1, b : b + BS].reshape(rows, channels)
        total = total + matmul(window, ws[1, b])
    current[...] = total
    arrive(halo[:2] + halo[4:])

    half = channels // 2

    def back_copy(k, h):
        peer = (me + k) % n
        return pltpu.make_async_remote_copy(
            src_ref=back.at[h, peer],
            dst_ref=returned.at[h, me],
            send_sem=back_sent.at[h, k],
            recv_sem=back_got.at[h, k],
            device_id={"tm": peer},
            device_id_type=mesh_id,
        )

    for h in range(2):
        part = slice(h * half, (h + 1) * half)
        total = current[:, part]
        for a in range(3):
            for b in range(3):
                if a != 1:
                    window = ext[a : a + BS, b : b + BS].reshape(rows, channels)
                    total = total + matmul(window, ws[a, b, :, part])
        back[h] = (
            matmul(by_frame, total.astype(jnp.bfloat16))
            .astype(jnp.bfloat16)
            .reshape(frames, BLOCK, half)
        )

        @pl.loop(1, n)
        def _(k):
            back_copy(k, h).start()

        returned[h, me] = back[h, me]

    to_window = one_hot(block_position(), PH * PW)

    @pl.loop(1, n)
    def _(k):
        in_copy(k).wait_send()

    for copy, there, comes in halo:

        @pl.when(there)
        def _():
            copy.wait_send()

    for h in range(2):

        @pl.loop(1, n)
        def _(k):
            back_copy(k, h).wait_recv()

        out[0, :, h * half : (h + 1) * half] = matmul(
            to_window, returned[h].reshape(PH * PW, half)
        ).astype(jnp.bfloat16)

    for h in range(2):

        @pl.loop(1, n)
        def _(k):
            back_copy(k, h).wait_send()


def block_body(latents, w_query, w_key, w_value, w_out, w_time, w_space, tile_starts):
    n = lax.axis_size("tm")
    channels = latents.shape[-1]
    vmem = pl.BlockSpec(memory_space=pltpu.VMEM)
    anywhere = pl.BlockSpec(memory_space=pltpu.HBM)
    dma = pltpu.SemaphoreType.DMA
    bf16 = jnp.bfloat16
    return pl.pallas_call(
        functools.partial(block_kernel, n=n),
        out_shape=jax.ShapeDtypeStruct(latents.shape, bf16),
        in_specs=[pl.BlockSpec(memory_space=pltpu.SMEM), vmem] + [anywhere] * 6,
        out_specs=vmem,
        scratch_shapes=[
            pltpu.VMEM(w_query.shape, bf16),
            pltpu.VMEM(w_key.shape, bf16),
            pltpu.VMEM(w_value.shape, bf16),
            pltpu.VMEM(w_out.shape, bf16),
            pltpu.VMEM(w_time.shape, bf16),
            pltpu.VMEM(w_space.shape, bf16),
            pltpu.VMEM((n, BLOCK, channels), bf16),
            pltpu.VMEM((n, BLOCK, channels), bf16),
            pltpu.VMEM((BS + 2, BS + 2, n, channels), bf16),
            pltpu.VMEM((2, n, BLOCK, channels // 2), bf16),
            pltpu.VMEM((2, n, BLOCK, channels // 2), bf16),
            pltpu.VMEM((n * BLOCK, channels), jnp.float32),
            dma((6,)),
            dma((n,)),
            dma((n,)),
            dma((8,)),
            dma((8,)),
            dma((2, n)),
            dma((2, n)),
        ],
        compiler_params=pltpu.CompilerParams(
            collective_id=0, has_side_effects=True, vmem_limit_bytes=60 * 2**20
        ),
    )(tile_starts, latents, w_query, w_key, w_value, w_out, w_time, w_space)


def any_body(latents, *rest):
    frames_dev, row_count, channels = latents.shape
    blocks = (PH // BS) * (PW // BS)
    if frames_dev == 1 and lax.axis_size("tm") == blocks and row_count == PH * PW:
        return block_body(latents, *rest)
    return body(latents, *rest)


def solution(mesh):
    placed = (P(("groups", "tm"), None, None), P(), P(), P(), P(), P(), P(), P("groups"))
    return jax.shard_map(
        any_body, mesh=mesh, in_specs=placed, out_specs=P(("groups", "tm"), None, None), check_vma=False
    )
```

```python
import functools

import jax
import jax.numpy as jnp
from jax import lax
from jax.experimental import pallas as pl
from jax.experimental.pallas import tpu as pltpu
from jax.sharding import PartitionSpec as P

PH = 16
PW = 32
OV = 2


epsilon = 1e-06


def passed_along(block, axis, distance):
    devices = range(lax.axis_size(axis))
    route = [(i - distance, i) for i in devices if i - distance in devices]
    return lax.ppermute(block, axis, route)


def rms_norm(array):
    wide = array.astype(jnp.float32)
    return (wide * lax.rsqrt(jnp.mean(wide * wide, axis=-1, keepdims=True) + epsilon)).astype(
        jnp.bfloat16
    )


def project(array, weight):
    extent = array.shape
    product = jnp.dot(array.reshape(-1, extent[-1]), weight, preferred_element_type=jnp.float32)
    return product.reshape(extent[:-1] + (weight.shape[-1],))


def tile_frames(frames, starts):
    reached = starts[None, :] <= frames[:, None]
    new_start = jnp.max(jnp.where(reached, starts[None, :], 0), axis=1)
    earlier = starts[None, :] < new_start[:, None]
    old_start = jnp.max(jnp.where(earlier, starts[None, :], 0), axis=1)
    inside = frames - new_start
    shared = jnp.logical_and(new_start > 0, inside < OV)
    fade = jnp.where(shared, (inside + 1).astype(jnp.float32) / float(OV + 1), jnp.float32(1.0))
    return (new_start, old_start, fade[:, None, None])


def attend(triple):
    queries, key_rows, values = triple
    length = queries.shape[0]
    scale = queries.shape[-1] ** (-0.5)
    scores = (
        jnp.einsum("fipc,gipc->ipfg", queries, key_rows, preferred_element_type=jnp.float32) * scale
    )
    order = jnp.arange(length)
    causal = order[:, None] >= order[None, :]
    scores = jnp.where(causal[None, None], scores, jnp.float32(-1e30))
    peak = jnp.max(scores, axis=-1, keepdims=True)
    expo = jnp.exp(scores - peak)
    weights = (expo / jnp.sum(expo, axis=-1, keepdims=True)).astype(jnp.bfloat16)
    return jnp.einsum(
        "ipfg,gipc->fipc", weights, values, preferred_element_type=jnp.float32
    ).astype(jnp.bfloat16)


def time_blend(padded, frames, starts, w_time):
    length = frames.shape[0]
    extent = padded.shape
    channels = extent[-1]
    flattened = padded.reshape(-1, channels)
    products = [
        jnp.dot(flattened, w_time[lag_index], preferred_element_type=jnp.float32).reshape(
            extent[0], -1, channels
        )
        for lag_index in range(3)
    ]
    new_start, old_start, fade = tile_frames(frames, starts)

    def mixed(context):
        summed = jnp.zeros((length,) + products[0].shape[1:], jnp.float32)
        for lag_index in range(3):
            actual = jnp.minimum(lag_index, frames - context)
            for delta_back in range(lag_index + 1):
                chosen = (actual == delta_back).astype(jnp.float32)[:, None, None]
                summed = (
                    summed + chosen * products[lag_index][2 - delta_back : 2 - delta_back + length]
                )
        return summed

    blended = fade * jax.nn.silu(mixed(new_start)) + (1.0 - fade) * jax.nn.silu(mixed(old_start))
    return blended.astype(jnp.bfloat16)


def space_mix(blended, hidden, w_space):
    length = blended.shape[0]
    channels = blended.shape[-1]
    spatial = blended.reshape(length, PH, PW, channels)
    padded = jnp.pad(spatial, ((0, 0), (1, 1), (1, 1), (0, 0)))
    summed = hidden.reshape(-1, channels).astype(jnp.float32)
    for row_shift in range(3):
        for col_shift in range(3):
            window = padded[:, row_shift : row_shift + PH, col_shift : col_shift + PW].reshape(
                -1, channels
            )
            summed = summed + jnp.dot(
                window, w_space[row_shift, col_shift], preferred_element_type=jnp.float32
            )
    return summed.reshape(length, PH * PW, channels).astype(jnp.bfloat16)


def body(latents, w_query, w_key, w_value, w_out, w_time, w_space, tile_starts):
    frames_dev, row_count, channels = latents.shape
    devices_tm = lax.axis_size("tm")
    share = row_count // devices_tm
    normed = rms_norm(latents).reshape(frames_dev, devices_tm, share, channels)
    queries = project(normed, w_query).astype(jnp.bfloat16)
    key_rows = project(normed, w_key).astype(jnp.bfloat16)
    values = project(normed, w_value).astype(jnp.bfloat16)
    attended = attend(
        (
            lax.all_to_all(queries, "tm", split_axis=1, concat_axis=0, tiled=True),
            lax.all_to_all(key_rows, "tm", split_axis=1, concat_axis=0, tiled=True),
            lax.all_to_all(values, "tm", split_axis=1, concat_axis=0, tiled=True),
        )
    )
    attended = lax.all_to_all(attended, "tm", split_axis=0, concat_axis=1, tiled=True).reshape(
        frames_dev, row_count, channels
    )
    hidden = (latents.astype(jnp.float32) + project(attended, w_out)).astype(jnp.bfloat16)
    smooth = rms_norm(hidden)
    reach = (frames_dev + 1) // frames_dev
    pieces = [passed_along(smooth, "tm", stride) for stride in range(reach, 0, -1)]
    earlier = jnp.concatenate(pieces, axis=0)
    offset = lax.axis_index("tm") * frames_dev
    frames = offset + jnp.arange(frames_dev)
    blended = time_blend(jnp.concatenate([earlier, smooth], axis=0), frames, tile_starts, w_time)
    return space_mix(blended, hidden, w_space)


BS = 4
BLOCK = BS * BS
GROUP = 128


def iota(shape, dim):
    return lax.broadcasted_iota(jnp.int32, shape, dim)


def one_hot(target, columns):
    rows = target.shape[0]
    return (jnp.broadcast_to(target, (rows, columns)) == iota((rows, columns), 1)).astype(
        jnp.float32
    ).astype(jnp.bfloat16)


def matmul(left, right):
    return jnp.dot(left, right, preferred_element_type=jnp.float32)


def place_of(device):
    core, x, y, z = device % 2, (device // 2) % 2, (device // 4) % 2, device // 8
    return 2 * y + (x + y) % 2, 2 * z + core


def device_at(row, column):
    y = row // 2
    return (column // 2) * 8 + y * 4 + ((row % 2 + y) % 2) * 2 + column % 2


def window_position():
    r = iota((PH * PW, 1), 0)
    device, q = r >> 4, r & 15
    core, x, y, z = device & 1, (device >> 1) & 1, (device >> 2) & 1, device >> 3
    row, column = 2 * y + (x ^ y), 2 * z + core
    return (row * BS + (q >> 2)) * PW + column * BS + (q & 3)


def block_position():
    p = iota((PH * PW, 1), 0)
    py, px = p >> 5, p & 31
    row, column = py >> 2, px >> 2
    y = row >> 1
    device = (column >> 1) * 8 + y * 4 + ((row & 1) ^ y) * 2 + (column & 1)
    return device * BLOCK + (py & 3) * BS + (px & 3)


def normalized(wide):
    scale = lax.rsqrt(jnp.mean(wide * wide, axis=-1, keepdims=True) + epsilon)
    return (wide * scale).astype(jnp.bfloat16)


def silu(v):
    return v / (1.0 + jnp.exp(-v))


def block_kernel(
    starts,
    latents,
    wq_any,
    wk_any,
    wv_any,
    wo_any,
    wt_any,
    ws_any,
    out,
    wq,
    wk,
    wv,
    wo,
    wt,
    ws,
    outgoing,
    arrived,
    ext,
    back,
    returned,
    current,
    weight_sem,
    sent,
    got,
    halo_sent,
    halo_got,
    back_sent,
    back_got,
    *,
    n,
):
    frames = n
    channels = latents.shape[-1]
    rows = BLOCK * frames
    me = lax.axis_index("tm")
    mesh_id = pl.DeviceIdType.MESH

    barrier = pltpu.get_barrier_semaphore()

    @pl.loop(1, n)
    def _(k):
        pl.semaphore_signal(
            barrier, inc=1, device_id={"tm": (me + k) % n}, device_id_type=mesh_id
        )

    weights = [
        pltpu.make_async_copy(source, target, weight_sem.at[i])
        for i, (source, target) in enumerate(
            ((wq_any, wq), (wk_any, wk), (wv_any, wv), (wo_any, wo), (wt_any, wt), (ws_any, ws))
        )
    ]
    for copy in weights:
        copy.start()

    outgoing[...] = (
        matmul(one_hot(window_position(), PH * PW), latents[0])
        .astype(jnp.bfloat16)
        .reshape(n, BLOCK, channels)
    )
    pl.semaphore_wait(barrier, n - 1)

    def in_copy(k):
        peer = (me + k) % n
        return pltpu.make_async_remote_copy(
            src_ref=outgoing.at[peer],
            dst_ref=arrived.at[me],
            send_sem=sent.at[k],
            recv_sem=got.at[k],
            device_id={"tm": peer},
            device_id_type=mesh_id,
        )

    @pl.loop(1, n)
    def _(k):
        in_copy(k % 2 * ((k + 1) // 2) + (1 - k % 2) * (n - k // 2)).start()

    arrived[me] = outgoing[me]

    row, column = place_of(me)
    edge = jnp.zeros((BS + 2, frames, channels), jnp.bfloat16)

    @pl.when(row == 0)
    def _():
        ext[0] = edge

    @pl.when(row == PH // BS - 1)
    def _():
        ext[BS + 1] = edge

    @pl.when(column == 0)
    def _():
        for i in range(BS + 2):
            ext[i, 0] = edge[0]

    @pl.when(column == PW // BS - 1)
    def _():
        for i in range(BS + 2):
            ext[i, BS + 1] = edge[0]

    r = iota((GROUP, 1), 0)
    frame = r % frames
    base = r - frame
    new_start = jnp.zeros((GROUP, 1), jnp.int32)
    for t in range(starts.shape[0]):
        new_start = jnp.maximum(new_start, jnp.where(frame >= starts[t], starts[t], 0))
    old_start = jnp.zeros((GROUP, 1), jnp.int32)
    for t in range(starts.shape[0]):
        old_start = jnp.maximum(old_start, jnp.where(new_start > starts[t], starts[t], 0))
    inside = frame - new_start
    fade = jnp.where(
        jnp.logical_and(new_start > 0, inside < OV),
        (inside + 1).astype(jnp.float32) / float(OV + 1),
        jnp.float32(1.0),
    )
    lags = [
        [one_hot(base + jnp.maximum(frame - j, start), GROUP) for j in (1, 2)]
        for start in (new_start, old_start)
    ]
    other = iota((GROUP, GROUP), 1)
    wide_frame, wide_base = jnp.broadcast_to(frame, other.shape), jnp.broadcast_to(base, other.shape)
    seen = jnp.logical_and(other >= wide_base, other <= wide_base + wide_frame)

    flat = iota((rows, 1), 0)
    by_position = one_hot((flat % frames) * BLOCK + flat // frames, rows)
    by_frame = one_hot((flat % BLOCK) * frames + flat // BLOCK, rows)

    @pl.loop(1, n)
    def _(k):
        in_copy(k).wait_recv()

    held = matmul(by_position, arrived[...].reshape(rows, channels))
    normed = normalized(held)
    for copy in weights[:3]:
        copy.wait()
    queries = matmul(normed, wq[...]).astype(jnp.bfloat16)
    key_rows = matmul(normed, wk[...]).astype(jnp.bfloat16)
    values = matmul(normed, wv[...]).astype(jnp.bfloat16)
    attended = []
    for g in range(rows // GROUP):
        part = slice(g * GROUP, (g + 1) * GROUP)
        scores = lax.dot_general(
            queries[part],
            key_rows[part],
            (((1,), (1,)), ((), ())),
            preferred_element_type=jnp.float32,
        ) * (channels ** (-0.5))
        scores = jnp.where(seen, scores, jnp.float32(-1e30))
        expo = jnp.exp(scores - jnp.max(scores, axis=-1, keepdims=True))
        share = (expo / jnp.sum(expo, axis=-1, keepdims=True)).astype(jnp.bfloat16)
        attended.append(matmul(share, values[part]).astype(jnp.bfloat16))
    weights[3].wait()
    hidden = (held + matmul(jnp.concatenate(attended, axis=0), wo[...])).astype(jnp.bfloat16)
    smooth = normalized(hidden.astype(jnp.float32))

    weights[4].wait()
    current[...] = matmul(smooth, wt[0])
    lag_weights = wt[1:3].reshape(2 * channels, channels)
    mixes = []
    for pair in lags:
        lagged = jnp.concatenate(
            [
                jnp.concatenate(
                    [
                        matmul(lag, smooth[g * GROUP : (g + 1) * GROUP]).astype(jnp.bfloat16)
                        for lag in pair
                    ],
                    axis=1,
                )
                for g in range(rows // GROUP)
            ],
            axis=0,
        )
        mixes.append(current[...] + matmul(lagged, lag_weights))
    fade = jnp.concatenate([fade] * (rows // GROUP), axis=0)
    blended = (fade * silu(mixes[0]) + (1.0 - fade) * silu(mixes[1])).astype(jnp.bfloat16)
    ext[1 : BS + 1, 1 : BS + 1] = blended.reshape(BS, BS, frames, channels)

    def span(step, sending):
        if step == 0:
            return pl.ds(1, BS)
        if sending:
            return pl.ds(1 if step < 0 else BS, 1)
        return pl.ds(BS + 1 if step < 0 else 0, 1)

    halo = []
    for i, (down, right) in enumerate(
        ((-1, 0), (1, 0), (0, -1), (0, 1), (-1, -1), (-1, 1), (1, -1), (1, 1))
    ):
        to_row, to_column = row + down, column + right
        there = jnp.logical_and(
            jnp.logical_and(to_row >= 0, to_row < PH // BS),
            jnp.logical_and(to_column >= 0, to_column < PW // BS),
        )
        from_row, from_column = row - down, column - right
        comes = jnp.logical_and(
            jnp.logical_and(from_row >= 0, from_row < PH // BS),
            jnp.logical_and(from_column >= 0, from_column < PW // BS),
        )
        peer = device_at((to_row + PH // BS) % (PH // BS), (to_column + PW // BS) % (PW // BS))
        copy = pltpu.make_async_remote_copy(
            src_ref=ext.at[span(down, True), span(right, True)],
            dst_ref=ext.at[span(down, False), span(right, False)],
            send_sem=halo_sent.at[i],
            recv_sem=halo_got.at[i],
            device_id={"tm": peer},
            device_id_type=mesh_id,
        )
        halo.append((copy, there, comes))

    for copy, there, comes in halo:

        @pl.when(there)
        def _():
            copy.start()

    weights[5].wait()
    current[...] = hidden.astype(jnp.float32) + matmul(blended, ws[1, 1])

    def arrive(chosen):
        for copy, there, comes in chosen:

            @pl.when(comes)
            def _():
                copy.wait_recv()

    arrive(halo[2:4])
    total = current[...]
    for b in (0, 2):
        window = ext[1 : BS + 1, b : b + BS].reshape(rows, channels)
        total = total + matmul(window, ws[1, b])
    current[...] = total
    arrive(halo[:2] + halo[4:])

    half = channels // 2

    def back_copy(k, h):
        peer = (me + k) % n
        return pltpu.make_async_remote_copy(
            src_ref=back.at[h, peer],
            dst_ref=returned.at[h, me],
            send_sem=back_sent.at[h, k],
            recv_sem=back_got.at[h, k],
            device_id={"tm": peer},
            device_id_type=mesh_id,
        )

    for h in range(2):
        part = slice(h * half, (h + 1) * half)
        total = current[:, part]
        for a in range(3):
            for b in range(3):
                if a != 1:
                    window = ext[a : a + BS, b : b + BS].reshape(rows, channels)
                    total = total + matmul(window, ws[a, b, :, part])
        back[h] = (
            matmul(by_frame, total.astype(jnp.bfloat16))
            .astype(jnp.bfloat16)
            .reshape(frames, BLOCK, half)
        )

        @pl.loop(1, n)
        def _(k):
            back_copy(k % 2 * ((k + 1) // 2) + (1 - k % 2) * (n - k // 2), h).start()

        returned[h, me] = back[h, me]

    to_window = one_hot(block_position(), PH * PW)

    @pl.loop(1, n)
    def _(k):
        in_copy(k).wait_send()

    for copy, there, comes in halo:

        @pl.when(there)
        def _():
            copy.wait_send()

    for h in range(2):

        @pl.loop(1, n)
        def _(k):
            back_copy(k, h).wait_recv()

        out[0, :, h * half : (h + 1) * half] = matmul(
            to_window, returned[h].reshape(PH * PW, half)
        ).astype(jnp.bfloat16)

    for h in range(2):

        @pl.loop(1, n)
        def _(k):
            back_copy(k, h).wait_send()


def block_body(latents, w_query, w_key, w_value, w_out, w_time, w_space, tile_starts):
    n = lax.axis_size("tm")
    channels = latents.shape[-1]
    vmem = pl.BlockSpec(memory_space=pltpu.VMEM)
    anywhere = pl.BlockSpec(memory_space=pltpu.HBM)
    dma = pltpu.SemaphoreType.DMA
    bf16 = jnp.bfloat16
    return pl.pallas_call(
        functools.partial(block_kernel, n=n),
        out_shape=jax.ShapeDtypeStruct(latents.shape, bf16),
        in_specs=[pl.BlockSpec(memory_space=pltpu.SMEM), vmem] + [anywhere] * 6,
        out_specs=vmem,
        scratch_shapes=[
            pltpu.VMEM(w_query.shape, bf16),
            pltpu.VMEM(w_key.shape, bf16),
            pltpu.VMEM(w_value.shape, bf16),
            pltpu.VMEM(w_out.shape, bf16),
            pltpu.VMEM(w_time.shape, bf16),
            pltpu.VMEM(w_space.shape, bf16),
            pltpu.VMEM((n, BLOCK, channels), bf16),
            pltpu.VMEM((n, BLOCK, channels), bf16),
            pltpu.VMEM((BS + 2, BS + 2, n, channels), bf16),
            pltpu.VMEM((2, n, BLOCK, channels // 2), bf16),
            pltpu.VMEM((2, n, BLOCK, channels // 2), bf16),
            pltpu.VMEM((n * BLOCK, channels), jnp.float32),
            dma((6,)),
            dma((n,)),
            dma((n,)),
            dma((8,)),
            dma((8,)),
            dma((2, n)),
            dma((2, n)),
        ],
        compiler_params=pltpu.CompilerParams(
            collective_id=0, has_side_effects=True, vmem_limit_bytes=60 * 2**20
        ),
    )(tile_starts, latents, w_query, w_key, w_value, w_out, w_time, w_space)


def any_body(latents, *rest):
    frames_dev, row_count, channels = latents.shape
    blocks = (PH // BS) * (PW // BS)
    if frames_dev == 1 and lax.axis_size("tm") == blocks and row_count == PH * PW:
        return block_body(latents, *rest)
    return body(latents, *rest)


def solution(mesh):
    placed = (P(("groups", "tm"), None, None), P(), P(), P(), P(), P(), P(), P("groups"))
    return jax.shard_map(
        any_body, mesh=mesh, in_specs=placed, out_specs=P(("groups", "tm"), None, None), check_vma=False
    )
```
